32 devices in a mesh: row: 4 (over y, x), col: 8 (over z, core).
Axes of the slice: x: 2, y: 2, z: 4, core: 2. Of those that a mesh axis runs over, the one named last changes fastest.
Arguments:
- tokens: bfloat16 [1024, 53248], P(('row', 'col')), may hold values from -6 to 6
- eigvecs: float32 [53248, 2048], P('row', 'col'), may hold values from -0.02734375 to 0.02734375
- eigvals: float32 [2048], P('col'), may hold values from 0.25 to 4
- v_first: float32 [53248, 256], P(('row', 'col')), may hold values from -0.109375 to 0.109375
- v_second: float32 [53248, 256], P(('row', 'col')), may hold values from -0.109375 to 0.109375
- t_first: float32 [256, 256], replicated, may hold values from -0.375 to 0.375
- t_second: float32 [256, 256], replicated, may hold values from -0.375 to 0.375
Outputs:
- whitened: float32 [1024, 2048], P('row', 'col')
The draws below stay inside these ranges and needn't reach their ends.
All inputs are finite; a program needn't handle non-finite values.
Results may differ from the reference program's by a relative error of at most 0.0029.
Values may be sent and summed in bfloat16 or wider, within the bound.
No kernel may reach another device: no remote copies, remote signals or barrier semaphores. Data moves between devices by JAX's collectives and lax.ppermute only.
A program may use at most 128 MiB of HBM per device.

```python
import math
import jax
import jax.numpy as jnp
from jax import lax

D = 53248
K = 2048
NB = 256
TOK = 1024


def shard_levels(own_key, dims, shards, smallest, top_value):
    loudness, own = 1.0, jax.random.fold_in(own_key, 6)
    for axis_at, parts in shards:
        heights = jnp.exp(jax.random.uniform(jax.random.fold_in(own, axis_at), (parts,), jnp.float32, smallest / len(shards), top_value / len(shards)))
        loudness = loudness * jnp.repeat(heights, dims[axis_at] // parts).reshape([-1 if axis == axis_at else 1 for axis in range(len(dims))])
    return loudness


def noise(own_key, shape, deviation, bound, split=(), held_as=jnp.bfloat16):
    values = jax.random.normal(own_key, shape, jnp.float32) * deviation
    if len(split) > 0:
        values = shard_levels(own_key, shape, split, -0.22, 0.18) * values
    return jnp.clip(values, min=-bound, max=bound).astype(held_as)


def setup_inputs(seed: int = 0) -> dict:
    splits = jax.random.split(jax.random.key(seed), 8)
    tokens = noise(splits[0], (TOK, D), 1.0, 6.0, ((0, 32),))
    eigvecs = noise(splits[1], (D, K), D ** -0.5, 0.02734375, ((0, 4), (1, 8)), jnp.float32)
    eigvals = jnp.clip(jnp.exp(math.log(4.0) - 2.7725887 * jax.random.uniform(splits[2], (K,), jnp.float32) ** shard_levels(splits[2], (K,), ((0, 8),), -0.2, 0.2)), 0.25, 4.0)
    v_first = noise(splits[3], (D, NB), (D // 16) ** -0.5, 0.109375, ((0, 32),), jnp.float32)
    v_second = noise(splits[4], (D, NB), (D // 16) ** -0.5, 0.109375, ((0, 32),), jnp.float32)
    t_first = noise(splits[5], (NB, NB), NB ** -0.5, 0.375, (), jnp.float32)
    t_second = noise(splits[6], (NB, NB), NB ** -0.5, 0.375, (), jnp.float32)
    return dict(tokens=tokens, eigvecs=eigvecs, eigvals=eigvals, v_first=v_first, v_second=v_second, t_first=t_first, t_second=t_second)


def reflect(block, panel, factor):
    inner = jnp.dot(panel.T, block, precision=lax.Precision.HIGHEST, preferred_element_type=jnp.float32)
    middle = jnp.dot(factor, inner, precision=lax.Precision.HIGHEST, preferred_element_type=jnp.float32)
    return block - jnp.dot(panel, middle, precision=lax.Precision.HIGHEST, preferred_element_type=jnp.float32)

def reference(tokens, eigvecs, eigvals, v_first, v_second, t_first, t_second):
    rotated = reflect(eigvecs, v_second, t_second)
    rotated = reflect(rotated, v_first, t_first)
    whitening = (rotated * lax.rsqrt(eigvals)[None, :]).astype(jnp.bfloat16)
    return jnp.dot(tokens, whitening, preferred_element_type=jnp.float32)
```

```python
import jax
import jax.numpy as jnp
from jax import lax
from jax.sharding import PartitionSpec as P

HIGHEST = lax.Precision.HIGHEST
CHUNKS = 2


def dot32(a, b):
    return jnp.dot(a, b, precision=HIGHEST, preferred_element_type=jnp.float32)


def dot16(a, b):
    return jnp.dot(a, b, preferred_element_type=jnp.float32)


def split(v):
    high = lax.reduce_precision(v, 8, 7)
    return high.astype(jnp.bfloat16), (v - high).astype(jnp.bfloat16)


def make(rows, cols):
    swap = [(i, i ^ 1) for i in range(cols)]
    groups = [[i for i in range(cols) if i % 2 == core] for core in range(2)]
    half = cols // 2

    def row_sum(x):
        return jnp.sum(lax.all_to_all(x, "row", split_axis=0, concat_axis=0, tiled=True), axis=0)

    def core_sum(parts, core):
        even = jnp.stack(parts[0::2])
        odd = jnp.stack(parts[1::2])
        mine = jnp.where(core == 0, even, odd)
        other = jnp.where(core == 0, odd, even)
        return mine + lax.ppermute(other, "col", swap)

    def z_sum(x):
        got = lax.all_to_all(x, "col", split_axis=0, concat_axis=0, tiled=True, axis_index_groups=groups)
        return jnp.sum(got, axis=0)

    def per_device(tokens, eigvecs, eigvals, v_first, v_second, t_first, t_second):
        nb = v_first.shape[1]
        core = lax.axis_index("col") % 2
        slab = lax.all_to_all(tokens, ("row", "col"), split_axis=1, concat_axis=0, tiled=True)
        tok = slab.shape[0]
        depth, width = v_first.shape[0], eigvecs.shape[1]
        high, low = split(jnp.concatenate([v_first, v_second], axis=1))
        along = dot16(slab, high) + dot16(slab, low)
        gram = dot32(v_first.T, v_second)
        packed = jnp.concatenate([
            along.reshape(rows, tok // rows, 2 * nb),
            jnp.broadcast_to(gram.reshape(1, nb // 2, 2 * nb), (rows, nb // 2, 2 * nb)),
        ], axis=1)
        packed = packed.reshape(rows * packed.shape[1], 2 * nb)
        packed = lax.psum(lax.psum_scatter(packed, "row", scatter_dimension=0, tiled=True), "col")
        along = packed[: tok // rows]
        gram = packed[tok // rows:].reshape(nb, nb)

        outs = []
        step = width // CHUNKS
        for j in range(CHUNKS):
            piece = eigvecs[:, j * step:(j + 1) * step].astype(jnp.bfloat16).reshape(cols, depth, step)
            piece = lax.all_to_all(piece, "col", split_axis=0, concat_axis=0, tiled=True)
            parts = []
            for s in range(cols):
                w = piece[s]
                p = dot16(slab, w)
                i = dot16(high.T, w) + dot16(low.T, w)
                parts.append(jnp.concatenate([p.reshape(rows, tok // rows, step), i.reshape(rows, 2 * nb // rows, step)], axis=1))
            summed = core_sum(parts, core)
            summed = row_sum(jnp.swapaxes(summed, 0, 1))
            summed = z_sum(summed)
            base = summed[: tok // rows]
            inner = summed[tok // rows:]
            inner = lax.all_to_all(jnp.broadcast_to(inner[None], (rows, *inner.shape)), "row", split_axis=0, concat_axis=0, tiled=True)
            inner = inner.reshape(2 * nb, step)
            m_second = dot32(t_second, inner[nb:])
            m_first = dot32(t_first, inner[:nb] - dot32(gram, m_second))
            scale = lax.rsqrt(eigvals[j * step:(j + 1) * step])
            outs.append((base - dot32(along[:, nb:], m_second) - dot32(along[:, :nb], m_first)) * scale[None, :])
        return jnp.concatenate(outs, axis=1)

    return per_device


def solution(mesh):
    in_specs = (
        P(("row", "col"), None),
        P("row", "col"),
        P("col"),
        P(("row", "col"), None),
        P(("row", "col"), None),
        P(),
        P(),
    )
    out_specs = P("row", "col")
    body = make(mesh.shape["row"], mesh.shape["col"])
    return jax.shard_map(body, mesh=mesh, in_specs=in_specs, out_specs=out_specs, check_vma=False)
```

```python
import functools

import jax
import jax.numpy as jnp
from jax import lax
from jax.experimental import pallas as pl
from jax.experimental.pallas import tpu as pltpu
from jax.sharding import PartitionSpec as P

HIGHEST = lax.Precision.HIGHEST
CUTS = (0.1875, 0.5625, 0.875, 1.0)
STEP = 16


def dot32(a, b):
    return jnp.dot(a, b, precision=HIGHEST, preferred_element_type=jnp.float32)


def dot_nt(a, b, precision=None):
    return lax.dot_general(a, b, (((1,), (1,)), ((), ())), precision=precision, preferred_element_type=jnp.float32)


def dot_nn(a, b):
    return jnp.dot(a, b, preferred_element_type=jnp.float32)


def split(v):
    high = lax.reduce_precision(v, 8, 7)
    return high.astype(jnp.bfloat16), (v - high).astype(jnp.bfloat16)


def after(x, earlier):
    return lax.optimization_barrier((x, earlier))[0]


def pick(x, i):
    return lax.dynamic_index_in_dim(x, i, axis=0, keepdims=False)


def turn_body(bounds, x_ref, *outs):
    for lo, hi, out in zip(bounds[:-1], bounds[1:], outs):
        out[0] = x_ref[:, lo:hi].T.astype(jnp.bfloat16)


def turn(x, bounds, blocks):
    depth, width = x.shape[0] // blocks, x.shape[1]
    sizes = [hi - lo for lo, hi in zip(bounds[:-1], bounds[1:])]
    return pl.pallas_call(
        functools.partial(turn_body, bounds),
        grid=(blocks,),
        in_specs=[pl.BlockSpec((depth, width), lambda i: (i, 0))],
        out_specs=[pl.BlockSpec((1, n, depth), lambda i: (i, 0, 0)) for n in sizes],
        out_shape=[jax.ShapeDtypeStruct((blocks, n, depth), jnp.bfloat16) for n in sizes],
        cost_estimate=pl.CostEstimate(flops=0, bytes_accessed=6 * x.size, transcendentals=0),
        name="turn",
    )(x)


def project_body(rows, order_ref, piece_ref, slab_ref, high_ref, low_ref, q_ref, *rest):
    outs, inner = rest[:rows], rest[rows]
    step = pl.program_id(0)

    @pl.when(step == 0)
    def _():
        piece = piece_ref[...]
        inner[...] = dot_nn(piece, high_ref[...]) + dot_nn(piece, low_ref[...])

    value = dot_nt(piece_ref[...], slab_ref[...]) - dot_nt(inner[...], q_ref[...], HIGHEST)
    for k in range(rows):
        @pl.when(step == k)
        def _():
            outs[k][...] = value


def project(order, piece, slab, high, low, q):
    rows = order.shape[0]
    count, depth = piece.shape
    mine, inner = slab.shape[0] // rows, q.shape[1]
    whole = lambda k, order: (0, 0)
    block = lambda k, order: (order[k], 0)
    return pl.pallas_call(
        functools.partial(project_body, rows),
        grid_spec=pltpu.PrefetchScalarGridSpec(
            num_scalar_prefetch=1,
            grid=(rows,),
            in_specs=[
                pl.BlockSpec((count, depth), whole),
                pl.BlockSpec((mine, depth), block),
                pl.BlockSpec((depth, inner), whole),
                pl.BlockSpec((depth, inner), whole),
                pl.BlockSpec((mine, inner), block),
            ],
            out_specs=[pl.BlockSpec((count, mine), whole)] * rows,
            scratch_shapes=[pltpu.VMEM((count, inner), jnp.float32)],
        ),
        out_shape=[jax.ShapeDtypeStruct((count, mine), jnp.float32)] * rows,
        cost_estimate=pl.CostEstimate(
            flops=2 * count * depth * (slab.shape[0] + 2 * inner) * 2,
            bytes_accessed=2 * (piece.size + slab.size + 2 * high.size) + 4 * count * slab.shape[0],
            transcendentals=0,
        ),
        name="project",
    )(order, piece, slab, high, low, q)


def make(rows, cols):
    half = cols // 2
    groups = [[i for i in range(cols) if i % 2 == core] for core in range(2)]

    def swap_core(x):
        return lax.ppermute(x, "col", [(i, i ^ 1) for i in range(cols)])

    def to_row(x, k):
        return lax.ppermute(x, "row", [(i, i ^ k) for i in range(rows)])

    def to_z(x, k):
        return lax.ppermute(x, "col", [(i, i ^ (2 * k)) for i in range(cols)])

    def row_sum(parts):
        got = [to_row(parts[k], k) for k in range(1, rows)]
        return sum(got, parts[0])

    def z_sum(parts):
        got = [to_z(parts[k], k) for k in range(1, half)]
        return sum(got, parts[0])

    def per_device(tokens, eigvecs, eigvals, v_first, v_second, t_first, t_second):
        nb = v_first.shape[1]
        row = lax.axis_index("row")
        core = lax.axis_index("col") % 2
        z = lax.axis_index("col") // 2
        width = eigvecs.shape[1]
        depth = v_first.shape[0]

        def in_core_order(mine, other, axis):
            return jnp.where(core == 0, jnp.concatenate([mine, other], axis), jnp.concatenate([other, mine], axis))

        raw = lax.all_to_all(tokens, ("row", "col"), split_axis=1, concat_axis=0, tiled=True)
        tok = raw.shape[0]
        mine = tok // rows
        v_own = jnp.concatenate([v_first, v_second], axis=1)
        v = in_core_order(v_own, swap_core(v_own), 0)
        v_high, v_low = split(v)
        gram = dot32(lax.dynamic_slice_in_dim(v[:, :nb], core * (nb // 2), nb // 2, 1).T, v[:, nb:])
        gram = gram.reshape(rows, nb // (4 * rows), 2 * nb)

        bounds = [0] + [min(width, -(-int(width * c) // STEP) * STEP) for c in CUTS]
        pieces = turn(eigvecs, bounds, half)
        raw, pieces, v_high, v_low, gram = lax.optimization_barrier((raw, pieces, v_high, v_low, gram))
        def send(piece, earlier):
            piece = after(piece, earlier)
            return lax.all_to_all(piece, "col", split_axis=0, concat_axis=0, tiled=True, axis_index_groups=groups)

        arrived = [send(pieces[0], raw)]
        slab = in_core_order(raw, swap_core(raw), 1)

        own = lax.dynamic_index_in_dim(slab.reshape(rows, 2, mine // 2, 2 * depth), core, 1, False)
        own = own.reshape(tok // 2, 2 * depth)
        along = (dot_nn(own, v_high) + dot_nn(own, v_low)).reshape(rows, mine // 2, 2 * nb)
        used = mine // 2 + gram.shape[1]
        pad = -used % (8 * half)
        packed = jnp.concatenate([along, gram, jnp.zeros((rows, pad, 2 * nb), jnp.float32)], axis=1)
        part = row_sum([pick(packed, row ^ k) for k in range(rows)]).reshape(half, (used + pad) // half, 2 * nb)
        total = z_sum([pick(part, z ^ k) for k in range(half)])
        got = jnp.stack([total] + [to_z(total, k) for k in range(1, half)])
        full = jnp.concatenate([pick(got, z ^ k) for k in range(half)], axis=0)
        earlier = full
        for piece in pieces[1:]:
            arrived.append(send(piece, (arrived[-1], earlier)))
            earlier = arrived[-1]
        both = jnp.stack([full] + [to_row(full, k) for k in range(1, rows)])
        both = jnp.stack([pick(both, row ^ k) for k in range(rows)])
        both_other = swap_core(both)
        gram = in_core_order(
            both[:, mine // 2: used].reshape(nb // 2, nb), both_other[:, mine // 2: used].reshape(nb // 2, nb), 0)
        along = in_core_order(both[:, : mine // 2], both_other[:, : mine // 2], 1).reshape(tok, 2 * nb)

        first = dot32(along[:, :nb], t_first)
        second = dot32(along[:, nb:] - dot32(first, gram), t_second)
        q = jnp.concatenate([first, second], axis=1)

        order = jnp.stack([row ^ k for k in range(rows)]).astype(jnp.int32)
        outs = []
        for piece in arrived:
            count = piece.shape[1]
            flat = piece.reshape(half * count, 2 * depth)
            part = row_sum(project(order, flat, slab, v_high, v_low, q))
            part = part.reshape(half, count, mine)
            outs.append(z_sum([pick(part, z ^ k) for k in range(half)]))
        return jnp.concatenate(outs, axis=0).T * lax.rsqrt(eigvals)[None, :]

    return per_device


def solution(mesh):
    in_specs = (
        P(("row", "col"), None),
        P("row", "col"),
        P("col"),
        P(("row", "col"), None),
        P(("row", "col"), None),
        P(),
        P(),
    )
    out_specs = P("row", "col")
    body = make(mesh.shape["row"], mesh.shape["col"])
    return jax.shard_map(body, mesh=mesh, in_specs=in_specs, out_specs=out_specs, check_vma=False)
```

```python
import functools

import jax
import jax.numpy as jnp
from jax import lax
from jax.experimental import pallas as pl
from jax.experimental.pallas import tpu as pltpu
from jax.sharding import PartitionSpec as P


HIGHEST = lax.Precision.HIGHEST
CUTS = (0.25, 0.375, 0.6875, 0.875, 1.0)
GROUPS = ((0, 1), (2,), (3,), (4,))
STEP = 16
KINDS = (jnp.float32, jnp.float32, jnp.float32)
VMEM = pl.BlockSpec(memory_space=pltpu.VMEM)
SMEM = pl.BlockSpec(memory_space=pltpu.SMEM)


def dot32(a, b):
    return jnp.dot(a, b, precision=HIGHEST, preferred_element_type=jnp.float32)


def dot_nt(a, b):
    return lax.dot_general(a, b, (((1,), (1,)), ((), ())), preferred_element_type=jnp.float32)


def dot_nn(a, b):
    return jnp.dot(a, b, preferred_element_type=jnp.float32)


def split(v):
    high = lax.reduce_precision(v, 8, 7)
    return high.astype(jnp.bfloat16), (v - high).astype(jnp.bfloat16)


def split_here(v):
    high = v.astype(jnp.bfloat16)
    return high, (v - high.astype(jnp.float32)).astype(jnp.bfloat16)


def after(x, earlier):
    return lax.optimization_barrier((x, earlier))[0]


def pick(x, i):
    return lax.dynamic_index_in_dim(x, i, axis=0, keepdims=False)


def turn_body(bounds, blocks, at_ref, x_ref, *outs):
    i = pl.program_id(0)
    for k in range(blocks):
        @pl.when(i == k)
        def _():
            for j, (lo, hi) in enumerate(zip(bounds[:-1], bounds[1:])):
                outs[j * blocks + k][0] = x_ref[:, lo:hi].T.astype(jnp.bfloat16)


def turn(at, x, bounds, blocks):
    depth, width = x.shape[0] // (2 * blocks), x.shape[1]
    sizes = [hi - lo for lo, hi in zip(bounds[:-1], bounds[1:])]

    def source(i, h, at):
        return (2 * lax.bitwise_xor(i, at[0]) + lax.bitwise_xor(h, at[1]), 0)

    def target(k):
        return lambda i, h, at: (jnp.clip(2 * (i - k) + h, 0, 1), 0, 0)

    outs = pl.pallas_call(
        functools.partial(turn_body, bounds, blocks),
        grid_spec=pltpu.PrefetchScalarGridSpec(
            num_scalar_prefetch=1,
            grid=(blocks, 2),
            in_specs=[pl.BlockSpec((depth, width), source)],
            out_specs=[pl.BlockSpec((1, n, depth), target(k)) for n in sizes for k in range(blocks)],
        ),
        out_shape=[jax.ShapeDtypeStruct((2, n, depth), jnp.bfloat16) for n in sizes for _ in range(blocks)],
        cost_estimate=pl.CostEstimate(flops=0, bytes_accessed=6 * x.size, transcendentals=0),
        name="turn",
    )(at, x)
    return [outs[j * blocks:(j + 1) * blocks] for j in range(len(sizes))]


def project_body(count_pieces, rows, last, order_ref, *refs):
    pieces, (raw, other, high, low, q) = refs[:count_pieces], refs[count_pieces:count_pieces + 5]
    outs = refs[count_pieces + 5:-5]
    piece_in, slab_in, v_in, q_in, sems = refs[-5:]
    _, depth = piece_in.shape[1:]
    starts = [0]
    for piece in pieces:
        starts.append(starts[-1] + piece.shape[1])
    mine = raw.shape[0] // rows
    count_in = [0]

    def stage(*moves):
        copies = []
        for source, target in moves:
            copies.append(pltpu.make_async_copy(source, target, sems.at[count_in[0]]))
            copies[-1].start()
            count_in[0] += 1
        return copies

    def slab(k):
        at = pl.ds(pl.multiple_of(order_ref[k] * mine, mine), mine)
        return stage((q.at[at], q_in.at[k]), (raw.at[at], slab_in.at[0, k]), (other.at[at], slab_in.at[1, k]))

    def wait(copies):
        for copy in copies:
            copy.wait()

    lead = stage(
        *[(p.at[h], piece_in.at[h, pl.ds(s, p.shape[1])]) for h in range(2) for p, s in zip(pieces, starts)],
        (high, v_in.at[0]))
    tail = stage((low, v_in.at[1]))
    wait(lead)
    ready = [slab(0)]
    own, rest = piece_in[0], piece_in[1]
    inner = dot_nn(own, v_in[0, :depth]) + dot_nn(rest, v_in[0, depth:])
    wait(tail)
    ready += [slab(k) for k in range(1, min(rows, 2))]
    inner = inner + dot_nn(own, v_in[1, :depth]) + dot_nn(rest, v_in[1, depth:])
    u_high, u_low = split_here(inner)
    for k in range(rows):
        wait(ready[k])
        if k + 2 < rows:
            ready.append(slab(k + 2))
        q_high, q_low = split_here(q_in[k])
        change = dot_nt(u_high, q_high) + dot_nt(u_high, q_low) + dot_nt(u_low, q_high)
        value = dot_nt(own, slab_in[0, k]) + dot_nt(rest, slab_in[1, k]) - change
        if not last:
            outs[k][...] = value.astype(outs[k].dtype)
            continue
        for i, (lo, hi) in enumerate(zip(starts[:-1], starts[1:])):
            outs[0][k, order_ref[rows + i]] = value[lo:hi].astype(outs[0].dtype)


def project(order, pieces, raw, other, high, low, q, rows, sent, last=False):
    _, count, depth = pieces[0].shape
    mine, inner = raw.shape[0] // rows, q.shape[1]
    size = sum(piece.shape[1] for piece in pieces)
    anywhere = pl.BlockSpec(memory_space=pl.ANY)
    if last:
        shapes = [jax.ShapeDtypeStruct((rows, len(pieces), count, mine), sent)]
    else:
        shapes = [jax.ShapeDtypeStruct((size, mine), jnp.float32 if k == 0 else sent) for k in range(rows)]
    return pl.pallas_call(
        functools.partial(project_body, len(pieces), rows, last),
        in_specs=[SMEM] + [anywhere] * (len(pieces) + 5),
        out_specs=[VMEM] * len(shapes),
        out_shape=shapes,
        scratch_shapes=[
            pltpu.VMEM((2, size, depth), jnp.bfloat16),
            pltpu.VMEM((2, rows, mine, depth), jnp.bfloat16),
            pltpu.VMEM((2, 2 * depth, inner), jnp.bfloat16),
            pltpu.VMEM((rows, mine, inner), jnp.float32),
            pltpu.SemaphoreType.DMA((2 * len(pieces) + 3 * rows + 2,)),
        ],
        cost_estimate=pl.CostEstimate(
            flops=4 * size * depth * (raw.shape[0] + 2 * inner),
            bytes_accessed=4 * (size * depth + raw.size + high.size) + 4 * size * raw.shape[0],
            transcendentals=0,
        ),
        name="project",
    )(order, *pieces, raw, other, high, low, q)


def make(rows, cols):
    half = cols // 2
    wide = [[r * cols + 2 * z + core for r in range(rows) for z in range(half)] for core in range(2)]

    def swap_core(x):
        return lax.ppermute(x, "col", [(i, i ^ 1) for i in range(cols)])

    def to_row(x, k):
        return lax.ppermute(x, "row", [(i, i ^ k) for i in range(rows)])

    def to_z(x, k):
        return lax.ppermute(x, "col", [(i, i ^ (2 * k)) for i in range(cols)])

    def row_sum(parts):
        got = [to_row(parts[k], k) for k in range(1, rows)]
        return sum((g.astype(jnp.float32) for g in got), parts[0])

    def z_sum(parts):
        got = []
        for k in range(1, half):
            got.append(to_z(parts[k], k))
        return sum((g.astype(jnp.float32) for g in got), parts[0])

    def per_device(tokens, eigvecs, eigvals, v_first, v_second, t_first, t_second):
        nb = v_first.shape[1]
        row = lax.axis_index("row")
        core = lax.axis_index("col") % 2
        z = lax.axis_index("col") // 2
        width = eigvecs.shape[1]

        raw = lax.all_to_all(tokens, ("row", "col"), split_axis=1, concat_axis=0, tiled=True)
        tok = raw.shape[0]
        mine = tok // rows
        part_rows = mine // 2
        gram_rows = nb // (4 * rows)
        v_own = jnp.concatenate([v_first, v_second], axis=1)
        v_rest = swap_core(v_own)
        v_high, v_low = split(jnp.concatenate([v_own, v_rest], axis=0))
        depth = v_own.shape[0]
        gram = dot32(v_first.T, v_second).reshape(2, rows, gram_rows, 2 * nb)

        bounds = [0] + [min(width, -(-int(width * c) // STEP) * STEP) for c in CUTS]
        pieces = turn(jnp.stack([z, core]).astype(jnp.int32), eigvecs, bounds, half)
        far = sorted(range(1, half), key=lambda k: -(k & (half // 2)))

        def send(j, earlier):
            piece, got = pieces[j], {}
            for k in far:
                got[k] = to_z(piece[k] if earlier is None else after(piece[k], earlier), k)
            return [piece[0]] + [got[k] for k in range(1, half)]

        raw, pieces, v_high, v_low, gram = lax.optimization_barrier((raw, pieces, v_high, v_low, gram))
        arrived = [send(0, raw)]
        other = swap_core(raw)

        along = dot_nn(raw, v_high[:depth]) + dot_nn(raw, v_low[:depth])
        along = jnp.swapaxes(along.reshape(rows, 2, part_rows, 2 * nb), 0, 1)
        used = part_rows + gram_rows
        pad = -used % (8 * half)
        packed = jnp.concatenate([along, gram], axis=2)
        packed = pick(packed, core) + swap_core(pick(packed, 1 - core))
        part = row_sum([pick(packed, row ^ k) for k in range(rows)])
        part = jnp.pad(part, ((0, pad), (0, 0))).reshape(half, (used + pad) // half, 2 * nb)
        total = z_sum([pick(part, z ^ k) for k in range(half)])
        arrived.append(send(1, part))
        got = [total]
        for k in range(1, half):
            got.append(to_z(total, k))
        got = jnp.stack(got)
        full = jnp.concatenate([pick(got, z ^ k) for k in range(half)], axis=0)
        arrived.append(send(2, full))
        both = [full]
        for k in range(1, rows):
            both.append(to_row(full, k))
        both = jnp.stack(both)
        both = jnp.stack([pick(both, row ^ k) for k in range(rows)])
        both_other = swap_core(both)

        def in_core_order(a, b, axis):
            return jnp.where(core == 0, jnp.concatenate([a, b], axis), jnp.concatenate([b, a], axis))

        gram = in_core_order(
            both[:, part_rows:used].reshape(nb // 2, nb), both_other[:, part_rows:used].reshape(nb // 2, nb), 0)
        along = in_core_order(both[:, :part_rows], both_other[:, :part_rows], 1).reshape(tok, 2 * nb)
        first = dot32(along[:, :nb], t_first)
        second = dot32(along[:, nb:] - dot32(first, gram), t_second)
        q = jnp.concatenate([first, second], axis=1)

        near = jnp.stack([row ^ k for k in range(rows)]).astype(jnp.int32)
        plain = jnp.concatenate([jnp.arange(rows), jnp.stack([z ^ k for k in range(half)])]).astype(jnp.int32)

        def chunk(g, order, sent, earlier, last=False):
            ready = q if earlier is None else after(q, earlier)
            flat = [piece for j in GROUPS[g] for piece in arrived[j]]
            return project(order, flat, raw, other, v_high, v_low, ready, rows, sent, last)

        def of_z(x, g):
            parts, at = [[] for _ in range(half)], 0
            for j in GROUPS[g]:
                n = bounds[j + 1] - bounds[j]
                for k in range(half):
                    parts[k].append(x[at:at + n])
                    at += n
            return [p[0] if len(p) == 1 else jnp.concatenate(p, axis=0) for p in parts]

        sums = []
        parts = None
        for g, sent in enumerate(KINDS):
            if g < 2:
                arrived.append(send(g + 3, parts or q))
            parts = chunk(g, near, sent, parts)
            sums.append(of_z(row_sum(parts), g))
        whole = [jnp.concatenate(p, axis=0) for p in zip(*sums)]
        last, = chunk(len(KINDS), plain, jnp.bfloat16, parts, True)
        last = last.reshape(rows * half, -1, mine)
        whole = z_sum(whole[:1] + [p.astype(jnp.bfloat16) for p in whole[1:]])
        last = lax.all_to_all(last, ("row", "col"), split_axis=0, concat_axis=0, tiled=True, axis_index_groups=wide)
        rest = jnp.sum(last.astype(jnp.float32), axis=0)
        return jnp.concatenate([whole, rest], axis=0).T * lax.rsqrt(eigvals)[None, :]

    return per_device


def solution(mesh):
    in_specs = (
        P(("row", "col"), None),
        P("row", "col"),
        P("col"),
        P(("row", "col"), None),
        P(("row", "col"), None),
        P(),
        P(),
    )
    out_specs = P("row", "col")
    body = make(mesh.shape["row"], mesh.shape["col"])

    return jax.shard_map(body, mesh=mesh, in_specs=in_specs, out_specs=out_specs, check_vma=False)
```
